256 devices in a mesh: grp: 16 (over x_hi, z), ing: 16 (over y, x_lo, core).
Axes of the slice: x: 4 (x_hi: 2, x_lo: 2; x = x_hi * 2 + x_lo), y: 4, z: 8, core: 2. Of those that a mesh axis runs over, the one named last changes fastest.
Arguments:
- state_vector: float32 [2, 16, 16, 131072], P(None, 'grp', 'ing'), may hold values from -6 to 6
- local_gates: float32 [2, 2, 32, 32], replicated, may hold values from -0.75 to 0.75
- local_angles: float32 [10], replicated, may hold values from -1 to 1
- pair_qubits: int32 [16, 2], replicated, may hold values from 0 to 9
- pair_angles: float32 [16], replicated, may hold values from -1 to 1
- group_gates: float32 [4, 2, 4, 4], replicated, may hold values from -2 to 2
- inner_gate: float32 [2, 32, 32], replicated, may hold values from -0.75 to 0.75
Outputs:
- new_state: float32 [2, 16, 16, 131072], P(None, 'grp', 'ing')
The draws below stay inside these ranges and needn't reach their ends.
Inputs may be any that keep to these rules, and one draw needn't show every extreme that they name: `pair_qubits`: qubit numbers; a pair may name one qubit twice.
All inputs are finite; a program needn't handle non-finite values.
Results may differ from the reference program's by a relative error of at most 0.00011.
Values sent between devices are 32-bit elements; how exact they have to be, the bound alone decides.
No kernel may reach another device: no remote copies, remote signals or barrier semaphores. Data moves between devices by JAX's collectives and lax.ppermute only.
A program may use at most 64 MiB of HBM per device.

```python
import jax
import jax.numpy as jnp
from jax import lax

AMPS_DEV = 131072
PHASE_QUBITS = 10
PAIRS = 16
GROUP_BITS = 4
N_GRP = 16
N_ING = 16


def set_ends(drawn, key, smallest, top_value):
    index_at = [jax.random.randint(jax.random.fold_in(key, axis), (), 0, length) for axis, length in enumerate(drawn.shape)]
    main_axis = drawn.shape.index(max(drawn.shape))
    beside = index_at[:main_axis] + [(index_at[main_axis] + 1) % drawn.shape[main_axis]] + index_at[main_axis + 1:]
    return drawn.at[tuple(index_at)].set(smallest).at[tuple(beside)].set(top_value)


def levels(own_key, shape, pieces, smallest, high):
    def one(dim, shards_of):
        heights = jax.random.uniform(jax.random.fold_in(jax.random.fold_in(own_key, 6), dim), (shards_of,), jnp.float32, smallest / len(pieces), high / len(pieces))
        return jnp.repeat(jnp.exp(heights), shape[dim] // shards_of).reshape((-1,) + (1,) * (len(shape) - dim - 1))

    level = one(*pieces[0])
    for cut in pieces[1:]:
        level = level * one(*cut)
    return level


def scatter_about(own_key, shape, deviation, reach, pieces=(), dtype=jnp.bfloat16):
    values = deviation * jax.random.normal(own_key, shape, jnp.float32)
    if pieces:
        values = values * levels(own_key, shape, pieces, -0.22, 0.18)
    return jnp.clip(values, -reach, reach).astype(dtype)


def setup_inputs(seed: int = 0) -> dict:
    keys = jax.random.split(jax.random.key(seed), 8)
    return {
        "state_vector": scatter_about(keys[0], (2, N_GRP, N_ING, AMPS_DEV), 1.0, 6.0, ((1, 16), (2, 16)), jnp.float32),
        "local_gates": scatter_about(keys[1], (2, 2, 32, 32), 64 ** -0.5, 0.75, (), jnp.float32),
        "local_angles": jnp.clip(jax.random.uniform(keys[2], (PHASE_QUBITS,), jnp.float32, -1.0, 1.0), -1.0, 1.0),
        "pair_qubits": set_ends(jax.random.randint(keys[3], (PAIRS, 2), 0, PHASE_QUBITS), jax.random.fold_in(keys[3], 1), 0, PHASE_QUBITS - 1).astype(jnp.int32),
        "pair_angles": jnp.clip(jax.random.uniform(keys[4], (PAIRS,), jnp.float32, -1.0, 1.0), -1.0, 1.0),
        "group_gates": scatter_about(keys[5], (GROUP_BITS, 2, 4, 4), 8 ** -0.5, 2.0, (), jnp.float32),
        "inner_gate": scatter_about(keys[6], (2, 32, 32), 64 ** -0.5, 0.75, (), jnp.float32),
    }


HIGHEST_PRECISION = lax.Precision.HIGHEST


def complex_apply(matrix, shaped, pattern):
    real_part = jnp.einsum(pattern, matrix[0], shaped[0], precision=HIGHEST_PRECISION) - jnp.einsum(pattern, matrix[1], shaped[1], precision=HIGHEST_PRECISION)
    imag_part = jnp.einsum(pattern, matrix[0], shaped[1], precision=HIGHEST_PRECISION) + jnp.einsum(pattern, matrix[1], shaped[0], precision=HIGHEST_PRECISION)
    return jnp.stack([real_part, imag_part])


def block_gate(flat, matrix, start):
    length = flat.shape[1]
    shaped = flat.reshape(2, length >> (start + 5), 32, 1 << start)
    return complex_apply(matrix, shaped, "ab,hbl->hal").reshape(2, length)


def pair_gate(flat, matrix, high_qubit, low_qubit):
    length = flat.shape[1]
    shaped = flat.reshape(2, length >> (high_qubit + 1), 2, 1 << (high_qubit - low_qubit - 1), 2, 1 << low_qubit)
    return complex_apply(matrix.reshape(2, 2, 2, 2, 2), shaped, "wxyz,hymzl->hwmxl").reshape(2, length)


def phase_angles(length, local_angles, pair_qubits, pair_angles):
    position = lax.iota(jnp.int32, length)
    phases = jnp.zeros((length,), jnp.float32)
    for qubit in range(local_angles.shape[0]):
        sign_value = (1 - 2 * ((position >> qubit) & 1)).astype(jnp.float32)
        phases = phases + local_angles[qubit] * sign_value
    for entry in range(pair_qubits.shape[0]):
        sign_first = 1 - 2 * ((position >> pair_qubits[entry, 0]) & 1)
        sign_second = 1 - 2 * ((position >> pair_qubits[entry, 1]) & 1)
        phases = phases + pair_angles[entry] * (sign_first * sign_second).astype(jnp.float32)
    return phases


def apply_phase(shaped, phases):
    cosine = jnp.cos(phases)
    sine = jnp.sin(phases)
    return jnp.stack([cosine * shaped[0] - sine * shaped[1], sine * shaped[0] + cosine * shaped[1]])


def reference(state_vector, local_gates, local_angles, pair_qubits, pair_angles, group_gates, inner_gate):
    local_bits = AMPS_DEV.bit_length() - 1
    inner_bits = N_ING.bit_length() - 1
    group_bits = N_GRP.bit_length() - 1
    flat = state_vector.reshape(2, -1)
    flat = block_gate(flat, local_gates[0], local_bits - 5)
    flat = block_gate(flat, local_gates[1], local_bits - 10)
    phases = phase_angles(AMPS_DEV, local_angles, pair_qubits, pair_angles)
    flat = apply_phase(flat.reshape(2, -1, AMPS_DEV), phases).reshape(2, -1)
    for level in range(group_bits):
        flat = pair_gate(flat, group_gates[level], local_bits + inner_bits + level, local_bits - 10 + level)
    flat = block_gate(flat, inner_gate, local_bits + inner_bits - 5)
    return flat.reshape(state_vector.shape)
```

```python
import jax
import jax.numpy as jnp
from jax import lax
from jax.experimental import pallas as pl
from jax.experimental.pallas import tpu as pltpu
from jax.sharding import PartitionSpec as P

F32 = jnp.float32
BF16 = jnp.bfloat16


def split(value):
    high = value.astype(BF16)
    return high, (value - high.astype(F32)).astype(BF16)


def dot(left, right, dims=((1,), (0,))):
    return lax.dot_general(left, right, (dims, ((), ())), preferred_element_type=F32)


def dot3(left, right, dims=((1,), (0,))):
    (left_high, left_low), (right_high, right_low) = left, right
    return (
        dot(left_high, right_high, dims)
        + dot(left_low, right_high, dims)
        + dot(left_high, right_low, dims)
    )


def prep_kernel(pair_ref, inner_ref, w_high, w_low, m_high, m_low):
    row = lax.broadcasted_iota(jnp.int32, (256, 8), 0)
    col = lax.broadcasted_iota(jnp.int32, (256, 8), 1)
    r_full = lax.broadcasted_iota(jnp.int32, (256, 256), 0)
    c_full = lax.broadcasted_iota(jnp.int32, (256, 256), 1)
    differ = jnp.bitwise_xor(r_full, c_full)
    for level in range(4):
        key = ((row >> 6) & 1) * 4 + (row >> 7) * 2 + ((row >> level) & 1)
        pick = (key == col).astype(F32).astype(BF16)
        keep = jnp.bitwise_and(differ, 63 - (1 << level)) == 0
        for part, out in zip(split(pair_ref[level]), (w_high, w_low)):
            half = dot(pick, part).astype(BF16)
            out[level] = jnp.where(keep, dot(half, pick, ((1,), (1,))), 0.0).astype(BF16)
    row = lax.broadcasted_iota(jnp.int32, (128, 32), 0)
    col = lax.broadcasted_iota(jnp.int32, (128, 32), 1)
    pick = ((row >> 2) == col).astype(F32).astype(BF16)
    keep = jnp.bitwise_and(differ[:128, :128], 3) == 0
    for c in range(2):
        for part, out in zip(split(inner_ref[c]), (m_high, m_low)):
            half = dot(pick, part).astype(BF16)
            out[c * 128 : c * 128 + 128] = jnp.where(keep, dot(half, pick, ((1,), (1,))), 0.0).astype(BF16)


def pre_kernel(angle_ref, qubit_ref, pair_ref, x_ref, gate_ref, out_ref, y_ref):
    real, imag = gate_ref[0, 0], gate_ref[0, 1]
    first = split(jnp.concatenate([jnp.concatenate([real, -imag], 1), jnp.concatenate([imag, real], 1)], 0))
    for start in range(0, 32, 8):
        columns = [x_ref[pl.ds(start + b, 64, stride=32), :] for b in range(8)]
        result = dot3(first, split(jnp.concatenate(columns, 1)))
        for b in range(8):
            y_ref[pl.ds(start + b, 64, stride=32), :] = result[:, b * 128 : b * 128 + 128]
    position = lax.broadcasted_iota(jnp.int32, (8, 128), 0) * 128 + lax.broadcasted_iota(jnp.int32, (8, 128), 1)
    phases = jnp.zeros((8, 128), F32)
    for qubit in range(10):
        phases = phases + angle_ref[qubit] * (1 - 2 * ((position >> qubit) & 1)).astype(F32)
    for entry in range(16):
        first_bit = lax.shift_right_logical(position, jnp.full((8, 128), qubit_ref[entry, 0], jnp.int32))
        second_bit = lax.shift_right_logical(position, jnp.full((8, 128), qubit_ref[entry, 1], jnp.int32))
        odd = jnp.bitwise_and(jnp.bitwise_xor(first_bit, second_bit), 1)
        phases = phases + pair_ref[entry] * (1 - 2 * odd).astype(F32)
    low = lax.broadcasted_iota(jnp.int32, (8, 128), 0)
    lane = lax.broadcasted_iota(jnp.int32, (8, 128), 1)
    spread = (low == jnp.bitwise_and(lane, 7)).astype(F32)
    signed = jnp.where(lane < 64, -spread, spread)

    def table(value, select):
        high, rest = split(value)
        select = select.astype(BF16)
        low_part = rest
        return dot(high, select, ((0,), (0,))) + dot(low_part, select, ((0,), (0,)))

    cosine = table(jnp.cos(phases), spread)
    sine = table(jnp.sin(phases), signed)
    real, imag = gate_ref[1, 0], gate_ref[1, 1]
    zero = jnp.zeros_like(real)
    rows = [
        [real, zero, -imag, zero],
        [zero, real, zero, -imag],
        [imag, zero, real, zero],
        [zero, imag, zero, real],
    ]
    second = jnp.concatenate([jnp.concatenate(r, 1) for r in rows], 0)
    second = split(second.T)
    sub = lax.broadcasted_iota(jnp.int32, (16, 8, 128), 1)
    for ah in range(8):
        halves = []
        for top in range(2):
            at = (top * 8 + ah) * 64
            x = jnp.concatenate([y_ref[at : at + 64], y_ref[1024 + at : 1024 + at + 64]], 0)
            z = dot3(split(x.T), second)
            z = cosine * z + sine * pltpu.roll(z, 64, 1)
            halves.append(z.reshape(16, 8, 128))
        z0, z1 = halves
        out_ref[ah, :, 0] = jnp.where(sub < 4, z0, pltpu.roll(z1, 4, 1))
        out_ref[ah, :, 1] = jnp.where(sub < 4, pltpu.roll(z0, 4, 1), z1)


def mid_kernel(x_ref, w_high, w_low, m_high, m_low, out_ref):
    inner = (m_high[...], m_low[...])
    lane = lax.broadcasted_iota(jnp.int32, (128, 128), 1)
    parts = []
    for g in range(16):
        u = dot3(inner, split(x_ref[g * 16 : g * 16 + 16].reshape(128, 128)))
        turned = pltpu.roll(u[128:], 64, 1)
        parts.append(u[:128] + jnp.where(lane < 64, -turned, turned))
    for level in range(4):
        weight = (w_high[level], w_low[level])
        new = [None] * 16
        for g in range(16):
            if g >> level & 1:
                continue
            h = g | 1 << level
            y = dot3(split(jnp.concatenate([parts[g], parts[h]], 1)), weight)
            new[g], new[h] = y[:, :128], y[:, 128:]
        parts = new
    for g in range(16):
        out_ref[g * 16 : g * 16 + 16] = parts[g].reshape(16, 8, 128)


def post_kernel(x_ref, out_ref):
    sub = lax.broadcasted_iota(jnp.int32, (16, 8, 128), 1)
    for ah in range(8):
        even, odd = x_ref[ah, :, 0], x_ref[ah, :, 1]
        z0 = jnp.where(sub < 4, even, pltpu.roll(odd, 4, 1)).reshape(128, 128)
        z1 = jnp.where(sub < 4, pltpu.roll(even, 4, 1), odd).reshape(128, 128)
        for top, z in enumerate((z0, z1)):
            at = (top * 8 + ah) * 64
            turned = z.T
            out_ref[at : at + 64] = turned[:64]
            out_ref[1024 + at : 1024 + at + 64] = turned[64:]


SMEM = pl.BlockSpec(memory_space=pltpu.SMEM)
VMEM = pl.BlockSpec(memory_space=pltpu.VMEM)
PARAMS = pltpu.CompilerParams(vmem_limit_bytes=48 << 20)


def on_device(state_vector, local_gates, local_angles, pair_qubits, pair_angles, group_gates, inner_gate):
    turned = group_gates.transpose(0, 1, 3, 2)
    real, imag = turned[:, 0], turned[:, 1]
    pairs = jnp.concatenate([jnp.concatenate([real, imag], 2), jnp.concatenate([-imag, real], 2)], 1)
    weights = pl.pallas_call(
        prep_kernel,
        out_shape=(
            jax.ShapeDtypeStruct((4, 256, 256), BF16),
            jax.ShapeDtypeStruct((4, 256, 256), BF16),
            jax.ShapeDtypeStruct((256, 128), BF16),
            jax.ShapeDtypeStruct((256, 128), BF16),
        ),
        in_specs=[VMEM, VMEM],
        out_specs=(VMEM,) * 4,
        compiler_params=PARAMS,
        name="prep",
    )(pairs, inner_gate)
    sent = pl.pallas_call(
        pre_kernel,
        out_shape=jax.ShapeDtypeStruct((8, 16, 2, 8, 128), F32),
        in_specs=[SMEM, SMEM, SMEM, VMEM, VMEM],
        out_specs=VMEM,
        scratch_shapes=[pltpu.VMEM((2048, 128), F32)],
        compiler_params=PARAMS,
        name="pre",
    )(local_angles, pair_qubits, pair_angles, state_vector.reshape(2048, 128), local_gates)
    held = lax.all_to_all(sent.reshape(256, 8, 128), ("grp", "ing"), 0, 0, tiled=True)
    done = pl.pallas_call(
        mid_kernel,
        out_shape=jax.ShapeDtypeStruct((256, 8, 128), F32),
        in_specs=[VMEM] * 5,
        out_specs=VMEM,
        compiler_params=PARAMS,
        name="mid",
    )(held, *weights)
    back = lax.all_to_all(done, ("grp", "ing"), 0, 0, tiled=True)
    out = pl.pallas_call(
        post_kernel,
        out_shape=jax.ShapeDtypeStruct((2048, 128), F32),
        in_specs=[VMEM],
        out_specs=VMEM,
        compiler_params=PARAMS,
        name="post",
    )(back.reshape(8, 16, 2, 8, 128))
    return out.reshape(state_vector.shape)


def solution(mesh):
    return jax.shard_map(
        on_device,
        mesh=mesh,
        in_specs=(P(None, "grp", "ing", None), P(), P(), P(), P(), P(), P()),
        out_specs=P(None, "grp", "ing", None),
        check_vma=False,
    )
```

```python
import jax
import jax.numpy as jnp
from jax import lax
from jax.experimental import pallas as pl
from jax.experimental.pallas import tpu as pltpu
from jax.sharding import PartitionSpec as P

F32 = jnp.float32
BF16 = jnp.bfloat16


def split(value):
    high = value.astype(BF16)
    return high, (value - high.astype(F32)).astype(BF16)


def dot(left, right, dims=((1,), (0,))):
    return lax.dot_general(left, right, (dims, ((), ())), preferred_element_type=F32)


def dot3(left, right, dims=((1,), (0,))):
    (left_high, left_low), (right_high, right_low) = left, right
    return (
        dot(left_high, right_high, dims)
        + dot(left_low, right_high, dims)
        + dot(left_high, right_low, dims)
    )


def prep_kernel(angle_ref, qubit_ref, twist_ref, pair_ref, inner_ref, w_high, w_low, m_high, m_low, turn_ref):
    row = lax.broadcasted_iota(jnp.int32, (256, 8), 0)
    col = lax.broadcasted_iota(jnp.int32, (256, 8), 1)
    r_full = lax.broadcasted_iota(jnp.int32, (256, 256), 0)
    c_full = lax.broadcasted_iota(jnp.int32, (256, 256), 1)
    differ = jnp.bitwise_xor(r_full, c_full)
    for level in range(4):
        key = ((row >> 6) & 1) * 4 + (row >> 7) * 2 + ((row >> level) & 1)
        pick = (key == col).astype(F32).astype(BF16)
        keep = jnp.bitwise_and(differ, 63 - (1 << level)) == 0
        for part, out in zip(split(pair_ref[level]), (w_high, w_low)):
            half = dot(pick, part).astype(BF16)
            out[level] = jnp.where(keep, dot(half, pick, ((1,), (1,))), 0.0).astype(BF16)
    row = lax.broadcasted_iota(jnp.int32, (128, 32), 0)
    col = lax.broadcasted_iota(jnp.int32, (128, 32), 1)
    pick = ((row >> 2) == col).astype(F32).astype(BF16)
    keep = jnp.bitwise_and(differ[:128, :128], 3) == 0
    for c in range(2):
        for part, out in zip(split(inner_ref[c]), (m_high, m_low)):
            half = dot(pick, part).astype(BF16)
            out[c * 128 : c * 128 + 128] = jnp.where(keep, dot(half, pick, ((1,), (1,))), 0.0).astype(BF16)
    base = (lax.axis_index("grp") & 1) * 64 + lax.axis_index("ing") * 4
    sub = lax.broadcasted_iota(jnp.int32, (8, 128), 0)
    lane = lax.broadcasted_iota(jnp.int32, (8, 128), 1)
    position = ((lane & 7) << 7) + (sub & 3) + base
    phases = jnp.zeros((8, 128), F32)
    for qubit in range(10):
        phases = phases + angle_ref[qubit] * (1 - 2 * ((position >> qubit) & 1)).astype(F32)
    for entry in range(16):
        first_bit = lax.shift_right_logical(position, jnp.full((8, 128), qubit_ref[0, entry], jnp.int32))
        second_bit = lax.shift_right_logical(position, jnp.full((8, 128), qubit_ref[1, entry], jnp.int32))
        odd = jnp.bitwise_and(jnp.bitwise_xor(first_bit, second_bit), 1)
        phases = phases + twist_ref[entry] * (1 - 2 * odd).astype(F32)
    turn_ref[0] = jnp.cos(phases)
    turn_ref[1] = jnp.sin(phases)


def pre_kernel(x_hbm, gate_hbm, z_ref, x_ref, gate_ref, y_ref, in_sems):
    fetch_gates = pltpu.make_async_copy(gate_hbm, gate_ref, in_sems.at[4])
    fetch_gates.start()
    x_view = x_ref.reshape(64, 32, 128)
    fetches = [
        pltpu.make_async_copy(x_hbm.at[:, pl.ds(8 * j, 8), :], x_view.at[:, pl.ds(8 * j, 8), :], in_sems.at[j])
        for j in range(4)
    ]
    for fetch in fetches:
        fetch.start()
    fetch_gates.wait()
    real, imag = gate_ref[0, 0], gate_ref[0, 1]
    first = split(jnp.concatenate([jnp.concatenate([real, -imag], 1), jnp.concatenate([imag, real], 1)], 0))
    real, imag = gate_ref[1, 0], gate_ref[1, 1]
    zero = jnp.zeros_like(real)
    rows = [
        [real, zero, -imag, zero],
        [zero, real, zero, -imag],
        [imag, zero, real, zero],
        [zero, imag, zero, real],
    ]
    second = split(jnp.concatenate([jnp.concatenate(r, 1) for r in rows], 0).T)
    for j in range(4):
        fetches[j].wait()
        columns = [x_ref[pl.ds(8 * j + b, 64, stride=32), :] for b in range(8)]
        result = dot3(first, split(jnp.concatenate(columns, 1)))
        for b in range(8):
            at = (8 * j + b) * 64
            y_ref[at : at + 64] = result[:, b * 128 : b * 128 + 128]
    sub = lax.broadcasted_iota(jnp.int32, (16, 8, 128), 1)
    for ah in range(8):
        halves = []
        for top in range(2):
            a = (top * 8 + ah) * 2
            x = jnp.concatenate([y_ref[pl.ds(c * 32 + a + q, 32, stride=64), :] for c in range(2) for q in range(2)], 0)
            halves.append(dot3(split(x.T), second).reshape(16, 8, 128))
        z0, z1 = halves
        z_ref[ah, :, 0] = jnp.where(sub < 4, z0, pltpu.roll(z1, 4, 1))
        z_ref[ah, :, 1] = jnp.where(sub < 4, pltpu.roll(z0, 4, 1), z1)


def mid_kernel(x_ref, w_high, w_low, m_high, m_low, turn_ref, out_ref):
    inner = (m_high[...], m_low[...])
    lane = lax.broadcasted_iota(jnp.int32, (128, 128), 1)
    cosine, sine = turn_ref[0], turn_ref[1]
    parts = []
    for g in range(16):
        u = dot3(inner, split(x_ref[g * 16 : g * 16 + 16].reshape(128, 128)))
        real, imag = u[:128].reshape(16, 8, 128), u[128:].reshape(16, 8, 128)
        kept = cosine * real - sine * imag
        turned = pltpu.roll((cosine * imag + sine * real).reshape(128, 128), 64, 1)
        parts.append(kept.reshape(128, 128) + jnp.where(lane < 64, -turned, turned))
    for level in range(4):
        weight = (w_high[level], w_low[level])
        new = [None] * 16
        for g in range(16):
            if g >> level & 1:
                continue
            h = g | 1 << level
            y = dot3(split(jnp.concatenate([parts[g], parts[h]], 1)), weight)
            new[g], new[h] = y[:, :128], y[:, 128:]
        parts = new
    for g in range(16):
        out_ref[g * 16 : g * 16 + 16] = parts[g].reshape(16, 8, 128)


def post_kernel(x_ref, out_hbm, z_ref, sems):
    sub = lax.broadcasted_iota(jnp.int32, (16, 8, 128), 1)
    sends = []
    for ah in range(8):
        even, odd = x_ref[ah, :, 0], x_ref[ah, :, 1]
        z0 = jnp.where(sub < 4, even, pltpu.roll(odd, 4, 1)).reshape(128, 128)
        z1 = jnp.where(sub < 4, pltpu.roll(even, 4, 1), odd).reshape(128, 128)
        for top, z in enumerate((z0, z1)):
            a = top * 8 + ah
            turned = z.T
            for c in range(2):
                at = c * 1024 + a * 64
                z_ref[at : at + 64] = turned[c * 64 : c * 64 + 64]
                send = pltpu.make_async_copy(
                    z_ref.at[pl.ds(at, 64)], out_hbm.at[pl.ds(at, 64)], sems.at[c * 16 + a]
                )
                send.start()
                sends.append(send)
    for send in sends:
        send.wait()


SMEM = pl.BlockSpec(memory_space=pltpu.SMEM)
VMEM = pl.BlockSpec(memory_space=pltpu.VMEM)
HBM = pl.BlockSpec(memory_space=pltpu.HBM)
PARAMS = pltpu.CompilerParams(vmem_limit_bytes=48 << 20)


def on_device(state_vector, local_gates, local_angles, pair_qubits, pair_angles, group_gates, inner_gate):
    turned = group_gates.transpose(0, 1, 3, 2)
    real, imag = turned[:, 0], turned[:, 1]
    pairs = jnp.concatenate([jnp.concatenate([real, imag], 2), jnp.concatenate([-imag, real], 2)], 1)
    weights = pl.pallas_call(
        prep_kernel,
        out_shape=(
            jax.ShapeDtypeStruct((4, 256, 256), BF16),
            jax.ShapeDtypeStruct((4, 256, 256), BF16),
            jax.ShapeDtypeStruct((256, 128), BF16),
            jax.ShapeDtypeStruct((256, 128), BF16),
            jax.ShapeDtypeStruct((2, 8, 128), F32),
        ),
        in_specs=[SMEM, SMEM, SMEM, VMEM, VMEM],
        out_specs=(VMEM,) * 5,
        compiler_params=PARAMS,
        name="prep",
    )(local_angles, pair_qubits.T, pair_angles, pairs, inner_gate)
    sent = pl.pallas_call(
        pre_kernel,
        out_shape=pltpu.VMEM((8, 16, 2, 8, 128), F32),
        in_specs=[HBM, HBM],
        out_specs=VMEM,
        scratch_shapes=[
            pltpu.VMEM((2048, 128), F32),
            pltpu.VMEM((2, 2, 32, 32), F32),
            pltpu.VMEM((2048, 128), F32),
            pltpu.SemaphoreType.DMA((5,)),
        ],
        compiler_params=PARAMS,
        name="pre",
    )(
        pltpu.with_memory_space_constraint(state_vector.reshape(64, 32, 128), pltpu.HBM),
        pltpu.with_memory_space_constraint(local_gates, pltpu.HBM),
    )
    held = lax.all_to_all(sent.reshape(256, 8, 128), ("grp", "ing"), 0, 0, tiled=True)
    done = pl.pallas_call(
        mid_kernel,
        out_shape=jax.ShapeDtypeStruct((256, 8, 128), F32),
        in_specs=[VMEM] * 6,
        out_specs=VMEM,
        compiler_params=PARAMS,
        name="mid",
    )(held, *weights)
    back = lax.all_to_all(done, ("grp", "ing"), 0, 0, tiled=True)
    out = pl.pallas_call(
        post_kernel,
        out_shape=jax.ShapeDtypeStruct((2048, 128), F32),
        in_specs=[VMEM],
        out_specs=HBM,
        scratch_shapes=[pltpu.VMEM((2048, 128), F32), pltpu.SemaphoreType.DMA((32,))],
        compiler_params=PARAMS,
        name="post",
    )(back.reshape(8, 16, 2, 8, 128))
    return out.reshape(state_vector.shape)


def solution(mesh):
    return jax.shard_map(
        on_device,
        mesh=mesh,
        in_specs=(P(None, "grp", "ing", None), P(), P(), P(), P(), P(), P()),
        out_specs=P(None, "grp", "ing", None),
        check_vma=False,
    )
```

```python
import jax
import jax.numpy as jnp
from jax import lax
from jax.experimental import pallas as pl
from jax.experimental.pallas import tpu as pltpu
from jax.sharding import PartitionSpec as P

F32 = jnp.float32
BF16 = jnp.bfloat16


def split(value):
    high = value.astype(BF16)
    return high, (value - high.astype(F32)).astype(BF16)


def dot(left, right, dims=((1,), (0,))):
    return lax.dot_general(left, right, (dims, ((), ())), preferred_element_type=F32)


def dot3(left, right, dims=((1,), (0,))):
    (left_high, left_low), (right_high, right_low) = left, right
    return (
        dot(left_high, right_high, dims)
        + dot(left_low, right_high, dims)
        + dot(left_high, right_low, dims)
    )


def prep_kernel(angle_ref, qubit_ref, twist_ref, pair_ref, inner_ref, w_high, w_low, m_high, m_low, turn_ref):
    row = lax.broadcasted_iota(jnp.int32, (256, 8), 0)
    col = lax.broadcasted_iota(jnp.int32, (256, 8), 1)
    r_full = lax.broadcasted_iota(jnp.int32, (256, 256), 0)
    c_full = lax.broadcasted_iota(jnp.int32, (256, 256), 1)
    differ = jnp.bitwise_xor(r_full, c_full)
    for high in range(2):
        halves = []
        for n in range(2):
            level = 2 * high + n
            group = (row >> 7) if n else (row >> 5) & 1
            key = ((row >> 6) & 1) * 4 + group * 2 + ((row >> level) & 1)
            pick = (key == col).astype(F32).astype(BF16)
            others = 255 - (64 + (128 if n else 32) + (1 << level))
            keep = jnp.bitwise_and(differ, others) == 0
            spread = []
            for part in split(pair_ref[level]):
                half = dot(pick, part).astype(BF16)
                spread.append(jnp.where(keep, dot(half, pick, ((1,), (1,))), 0.0).astype(BF16))
            halves.append(spread)
        w_high[high], w_low[high] = split(dot3(*halves))
    row = lax.broadcasted_iota(jnp.int32, (128, 32), 0)
    col = lax.broadcasted_iota(jnp.int32, (128, 32), 1)
    pick = ((row >> 2) == col).astype(F32).astype(BF16)
    keep = jnp.bitwise_and(differ[:128, :128], 3) == 0
    for c in range(2):
        for part, out in zip(split(inner_ref[c]), (m_high, m_low)):
            half = dot(pick, part).astype(BF16)
            out[c * 128 : c * 128 + 128] = jnp.where(keep, dot(half, pick, ((1,), (1,))), 0.0).astype(BF16)
    base = (lax.axis_index("grp") & 1) * 64 + lax.axis_index("ing") * 4
    sub = lax.broadcasted_iota(jnp.int32, (8, 128), 0)
    lane = lax.broadcasted_iota(jnp.int32, (8, 128), 1)
    position = ((lane & 7) << 7) + (sub & 3) + base
    phases = jnp.zeros((8, 128), F32)
    for qubit in range(10):
        phases = phases + angle_ref[qubit] * (1 - 2 * ((position >> qubit) & 1)).astype(F32)
    for entry in range(16):
        first_bit = lax.shift_right_logical(position, jnp.full((8, 128), qubit_ref[0, entry], jnp.int32))
        second_bit = lax.shift_right_logical(position, jnp.full((8, 128), qubit_ref[1, entry], jnp.int32))
        odd = jnp.bitwise_and(jnp.bitwise_xor(first_bit, second_bit), 1)
        phases = phases + twist_ref[entry] * (1 - 2 * odd).astype(F32)
    turn_ref[0] = jnp.cos(phases)
    turn_ref[1] = jnp.sin(phases)


def pre_kernel(x_hbm, gate_hbm, out_hbm, x_ref, gate_ref, y_ref, z_ref, in_sems, out_sems):
    fetch_gates = pltpu.make_async_copy(gate_hbm, gate_ref, in_sems.at[0])
    fetch_gates.start()
    fetch = pltpu.make_async_copy(x_hbm, x_ref, in_sems.at[1])
    fetch.start()
    fetch_gates.wait()
    real, imag = gate_ref[0, 0], gate_ref[0, 1]
    first = split(jnp.concatenate([jnp.concatenate([real, -imag], 1), jnp.concatenate([imag, real], 1)], 0))
    real, imag = gate_ref[1, 0], gate_ref[1, 1]
    zero = jnp.zeros_like(real)
    rows = [
        [real, zero, -imag, zero],
        [zero, real, zero, -imag],
        [imag, zero, real, zero],
        [zero, imag, zero, real],
    ]
    second = split(jnp.concatenate([jnp.concatenate(r, 1) for r in rows], 0).T)
    fetch.wait()
    for j in range(4):
        columns = [x_ref[pl.ds(8 * j + b, 64, stride=32), :] for b in range(8)]
        result = dot3(first, split(jnp.concatenate(columns, 1)))
        for b in range(8):
            at = (8 * j + b) * 64
            y_ref[at : at + 64] = result[:, b * 128 : b * 128 + 128]
    sub = lax.broadcasted_iota(jnp.int32, (16, 8, 128), 1)
    sends = []
    for ah in range(8):
        halves = []
        for top in range(2):
            a = (top * 8 + ah) * 2
            x = jnp.concatenate([y_ref[pl.ds(c * 32 + a + q, 32, stride=64), :] for c in range(2) for q in range(2)], 0)
            halves.append(dot3(split(x.T), second).reshape(16, 8, 128))
        z0, z1 = halves
        z_ref[ah, :, 0] = jnp.where(sub < 4, z0, pltpu.roll(z1, 4, 1))
        z_ref[ah, :, 1] = jnp.where(sub < 4, pltpu.roll(z0, 4, 1), z1)
        sends.append(pltpu.make_async_copy(z_ref.at[ah], out_hbm.at[ah], out_sems.at[ah]))
        sends[-1].start()
    for send in sends:
        send.wait()


def mid_kernel(x_ref, w_high, w_low, m_high, m_low, turn_ref, out_ref):
    inner = (m_high[...], m_low[...])
    lane = lax.broadcasted_iota(jnp.int32, (128, 128), 1)
    cosine, sine = turn_ref[0], turn_ref[1]
    parts = []
    for g in range(16):
        u = dot3(inner, split(x_ref[g * 16 : g * 16 + 16].reshape(128, 128)))
        real, imag = u[:128].reshape(16, 8, 128), u[128:].reshape(16, 8, 128)
        kept = cosine * real - sine * imag
        turned = pltpu.roll((cosine * imag + sine * real).reshape(128, 128), 64, 1)
        parts.append(kept.reshape(128, 128) + jnp.where(lane < 64, -turned, turned))
    low = (lane & 32) == 0

    def trade(first, second):
        return (
            jnp.where(low, first, pltpu.roll(second, 32, 1)),
            jnp.where(low, pltpu.roll(first, 96, 1), second),
        )

    def joined(first, second, level):
        y = dot3(split(jnp.concatenate([first, second], 1)), (w_high[level], w_low[level]))
        return y[:, :128], y[:, 128:]

    for g in range(0, 16, 2):
        parts[g], parts[g + 1] = trade(parts[g], parts[g + 1])
    for g in (0, 1, 4, 5, 8, 9, 12, 13):
        parts[g], parts[g + 2] = joined(parts[g], parts[g + 2], 0)
    for g in (0, 1, 2, 3, 8, 9, 10, 11):
        parts[g], parts[g + 4] = trade(parts[g], parts[g + 4])
    for g in range(8):
        parts[g], parts[g + 8] = joined(parts[g], parts[g + 8], 1)
    for g in range(0, 16, 2):
        parts[g], parts[g + 1] = trade(parts[g], parts[g + 1])
    for slot in range(16):
        g = (slot & 8) | (slot & 2) | ((slot & 1) << 2) | ((slot >> 2) & 1)
        out_ref[g * 16 : g * 16 + 16] = parts[slot].reshape(16, 8, 128)


def post_kernel(x_ref, out_hbm, z_ref, sems):
    sub = lax.broadcasted_iota(jnp.int32, (16, 8, 128), 1)
    sends = []
    for ah in range(8):
        even, odd = x_ref[ah, :, 0], x_ref[ah, :, 1]
        z0 = jnp.where(sub < 4, even, pltpu.roll(odd, 4, 1)).reshape(128, 128)
        z1 = jnp.where(sub < 4, pltpu.roll(even, 4, 1), odd).reshape(128, 128)
        for top, z in enumerate((z0, z1)):
            turned = z.T
            for c in range(2):
                z_ref[c, top, ah] = turned[c * 64 : c * 64 + 64]
        send = pltpu.make_async_copy(z_ref.at[:, :, ah], out_hbm.at[:, :, ah], sems.at[ah])
        send.start()
        sends.append(send)
    for send in sends:
        send.wait()


SMEM = pl.BlockSpec(memory_space=pltpu.SMEM)
VMEM = pl.BlockSpec(memory_space=pltpu.VMEM)
HBM = pl.BlockSpec(memory_space=pltpu.HBM)
PARAMS = pltpu.CompilerParams(vmem_limit_bytes=48 << 20)


def on_device(state_vector, local_gates, local_angles, pair_qubits, pair_angles, group_gates, inner_gate):
    turned = group_gates.transpose(0, 1, 3, 2)
    real, imag = turned[:, 0], turned[:, 1]
    pairs = jnp.concatenate([jnp.concatenate([real, imag], 2), jnp.concatenate([-imag, real], 2)], 1)
    weights = pl.pallas_call(
        prep_kernel,
        out_shape=(
            jax.ShapeDtypeStruct((2, 256, 256), BF16),
            jax.ShapeDtypeStruct((2, 256, 256), BF16),
            jax.ShapeDtypeStruct((256, 128), BF16),
            jax.ShapeDtypeStruct((256, 128), BF16),
            jax.ShapeDtypeStruct((2, 8, 128), F32),
        ),
        in_specs=[SMEM, SMEM, SMEM, VMEM, VMEM],
        out_specs=(VMEM,) * 5,
        compiler_params=PARAMS,
        name="prep",
    )(local_angles, pair_qubits.T, pair_angles, pairs, inner_gate)
    sent = pl.pallas_call(
        pre_kernel,
        out_shape=pltpu.HBM((8, 16, 2, 8, 128), F32),
        in_specs=[HBM, HBM],
        out_specs=HBM,
        scratch_shapes=[
            pltpu.VMEM((2048, 128), F32),
            pltpu.VMEM((2, 2, 32, 32), F32),
            pltpu.VMEM((2048, 128), F32),
            pltpu.VMEM((8, 16, 2, 8, 128), F32),
            pltpu.SemaphoreType.DMA((2,)),
            pltpu.SemaphoreType.DMA((8,)),
        ],
        compiler_params=PARAMS,
        name="pre",
    )(
        pltpu.with_memory_space_constraint(state_vector.reshape(2048, 128), pltpu.HBM),
        pltpu.with_memory_space_constraint(local_gates, pltpu.HBM),
    )
    held = lax.all_to_all(sent.reshape(256, 8, 128), ("grp", "ing"), 0, 0, tiled=True)
    done = pl.pallas_call(
        mid_kernel,
        out_shape=jax.ShapeDtypeStruct((256, 8, 128), F32),
        in_specs=[VMEM] * 6,
        out_specs=VMEM,
        compiler_params=PARAMS,
        name="mid",
    )(held, *weights)
    back = lax.all_to_all(done, ("grp", "ing"), 0, 0, tiled=True)
    out = pl.pallas_call(
        post_kernel,
        out_shape=pltpu.HBM((2, 2, 8, 64, 128), F32),
        in_specs=[VMEM],
        out_specs=HBM,
        scratch_shapes=[pltpu.VMEM((2, 2, 8, 64, 128), F32), pltpu.SemaphoreType.DMA((8,))],
        compiler_params=PARAMS,
        name="post",
    )(back.reshape(8, 16, 2, 8, 128))
    return out.reshape(state_vector.shape)


def solution(mesh):
    return jax.shard_map(
        on_device,
        mesh=mesh,
        in_specs=(P(None, "grp", "ing", None), P(), P(), P(), P(), P(), P()),
        out_specs=P(None, "grp", "ing", None),
        check_vma=False,
    )
```

```python
import jax
import jax.numpy as jnp
from jax import lax
from jax.experimental import pallas as pl
from jax.experimental.pallas import tpu as pltpu
from jax.sharding import PartitionSpec as P

F32 = jnp.float32
BF16 = jnp.bfloat16


def split(value):
    high = value.astype(BF16)
    return high, (value - high.astype(F32)).astype(BF16)


def dot(left, right, dims=((1,), (0,))):
    return lax.dot_general(left, right, (dims, ((), ())), preferred_element_type=F32)


def dot3(left, right, dims=((1,), (0,))):
    (left_high, left_low), (right_high, right_low) = left, right
    return (
        dot(left_high, right_high, dims)
        + dot(left_low, right_high, dims)
        + dot(left_high, right_low, dims)
    )


def prep_kernel(angle_ref, qubit_ref, twist_ref, pair_ref, inner_ref, w_high, w_low, m_high, m_low, turn_ref):
    row = lax.broadcasted_iota(jnp.int32, (256, 8), 0)
    col = lax.broadcasted_iota(jnp.int32, (256, 8), 1)
    r_full = lax.broadcasted_iota(jnp.int32, (256, 256), 0)
    c_full = lax.broadcasted_iota(jnp.int32, (256, 256), 1)
    differ = jnp.bitwise_xor(r_full, c_full)
    for high in range(2):
        halves = []
        for n in range(2):
            level = 2 * high + n
            group = (row >> 7) if n else (row >> 5) & 1
            key = ((row >> 6) & 1) * 4 + group * 2 + ((row >> level) & 1)
            pick = (key == col).astype(F32).astype(BF16)
            others = 255 - (64 + (128 if n else 32) + (1 << level))
            keep = jnp.bitwise_and(differ, others) == 0
            spread = []
            for part in split(pair_ref[level]):
                half = dot(pick, part).astype(BF16)
                spread.append(jnp.where(keep, dot(half, pick, ((1,), (1,))), 0.0).astype(BF16))
            halves.append(spread)
        w_high[high], w_low[high] = split(dot3(*halves))
    row = lax.broadcasted_iota(jnp.int32, (128, 32), 0)
    col = lax.broadcasted_iota(jnp.int32, (128, 32), 1)
    pick = ((row >> 2) == col).astype(F32).astype(BF16)
    keep = jnp.bitwise_and(differ[:128, :128], 3) == 0
    for c in range(2):
        for part, out in zip(split(inner_ref[c]), (m_high, m_low)):
            half = dot(pick, part).astype(BF16)
            out[:, c * 128 : c * 128 + 128] = jnp.where(keep, dot(half, pick, ((1,), (1,))), 0.0).astype(BF16)
    base = (lax.axis_index("grp") & 1) * 64 + lax.axis_index("ing") * 4
    sub = lax.broadcasted_iota(jnp.int32, (8, 128), 0)
    lane = lax.broadcasted_iota(jnp.int32, (8, 128), 1)
    position = ((lane & 7) << 7) + (sub & 3) + base
    phases = jnp.zeros((8, 128), F32)
    for qubit in range(10):
        phases = phases + angle_ref[qubit] * (1 - 2 * ((position >> qubit) & 1)).astype(F32)
    for entry in range(16):
        first_bit = lax.shift_right_logical(position, jnp.full((8, 128), qubit_ref[0, entry], jnp.int32))
        second_bit = lax.shift_right_logical(position, jnp.full((8, 128), qubit_ref[1, entry], jnp.int32))
        odd = jnp.bitwise_and(jnp.bitwise_xor(first_bit, second_bit), 1)
        phases = phases + twist_ref[entry] * (1 - 2 * odd).astype(F32)
    turn_ref[0] = jnp.cos(phases)
    turn_ref[1] = jnp.sin(phases)


def pre_kernel(x_hbm, gate_hbm, out_hbm, x_ref, gate_ref, y_ref, z_ref, in_sems, out_sems):
    fetch_gates = pltpu.make_async_copy(gate_hbm, gate_ref, in_sems.at[0])
    fetch_gates.start()
    fetch = pltpu.make_async_copy(x_hbm, x_ref, in_sems.at[1])
    fetch.start()
    fetch_gates.wait()
    real, imag = gate_ref[0, 0], gate_ref[0, 1]
    first = split(jnp.concatenate([jnp.concatenate([real, -imag], 1), jnp.concatenate([imag, real], 1)], 0))
    real, imag = gate_ref[1, 0], gate_ref[1, 1]
    zero = jnp.zeros_like(real)
    rows = [
        [real, zero, -imag, zero],
        [zero, real, zero, -imag],
        [imag, zero, real, zero],
        [zero, imag, zero, real],
    ]
    second = split(jnp.concatenate([jnp.concatenate(r, 1) for r in rows], 0).T)
    first_high, first_low = first
    stacked = jnp.concatenate([first_high, first_low, first_high], 1)
    fetch.wait()
    for j in range(4):
        columns = [x_ref[pl.ds(8 * j + b, 64, stride=32), :] for b in range(8)]
        high, rest = split(jnp.concatenate(columns, 1))
        result = dot(stacked, jnp.concatenate([high, high, rest], 0))
        for b in range(8):
            at = (8 * j + b) * 64
            y_ref[at : at + 64] = result[:, b * 128 : b * 128 + 128]
    sub = lax.broadcasted_iota(jnp.int32, (16, 8, 128), 1)
    sends = []
    for ah in range(8):
        halves = []
        for top in range(2):
            a = (top * 8 + ah) * 2
            x = jnp.concatenate([y_ref[pl.ds(c * 32 + a + q, 32, stride=64), :] for c in range(2) for q in range(2)], 0)
            halves.append(dot3(split(x.T), second).reshape(16, 8, 128))
        z0, z1 = halves
        z_ref[ah, :, 0] = jnp.where(sub < 4, z0, pltpu.roll(z1, 4, 1))
        z_ref[ah, :, 1] = jnp.where(sub < 4, pltpu.roll(z0, 4, 1), z1)
        sends.append(pltpu.make_async_copy(z_ref.at[ah], out_hbm.at[ah], out_sems.at[ah]))
        sends[-1].start()
    for send in sends:
        send.wait()


def mid_kernel(x_ref, w_high, w_low, m_high, m_low, turn_ref, out_ref):
    inner = (m_high[...], m_low[...])
    lane = lax.broadcasted_iota(jnp.int32, (128, 128), 1)
    cosine, sine = turn_ref[0], turn_ref[1]
    sign = jnp.where(lane[:8] < 64, -1.0, 1.0)
    cosine_i, sine_i = cosine * sign, sine * sign
    parts = []
    for start in range(0, 16, 2):
        columns = []
        for g in range(start, start + 2):
            x = x_ref[g * 16 : g * 16 + 16]
            swapped = pltpu.roll(x.reshape(128, 128), 64, 1).reshape(16, 8, 128)
            third = cosine * x + sine_i * swapped
            third_i = cosine_i * swapped - sine * x
            columns.append(jnp.concatenate([third.reshape(128, 128), third_i.reshape(128, 128)], 0))
        u = dot3(inner, split(jnp.concatenate(columns, 1)))
        parts += [u[:, :128], u[:, 128:]]
    low = (lane & 32) == 0

    def trade(first, second):
        return (
            jnp.where(low, first, pltpu.roll(second, 32, 1)),
            jnp.where(low, pltpu.roll(first, 96, 1), second),
        )

    def joined(first, second, level):
        y = dot3(split(jnp.concatenate([first, second], 1)), (w_high[level], w_low[level]))
        return y[:, :128], y[:, 128:]

    for g in range(0, 16, 2):
        parts[g], parts[g + 1] = trade(parts[g], parts[g + 1])
    for g in (0, 1, 4, 5, 8, 9, 12, 13):
        parts[g], parts[g + 2] = joined(parts[g], parts[g + 2], 0)
    for g in (0, 1, 2, 3, 8, 9, 10, 11):
        parts[g], parts[g + 4] = trade(parts[g], parts[g + 4])
    for g in range(8):
        parts[g], parts[g + 8] = joined(parts[g], parts[g + 8], 1)
    for g in range(0, 16, 2):
        parts[g], parts[g + 1] = trade(parts[g], parts[g + 1])
    for slot in range(16):
        g = (slot & 8) | (slot & 2) | ((slot & 1) << 2) | ((slot >> 2) & 1)
        out_ref[g * 16 : g * 16 + 16] = parts[slot].reshape(16, 8, 128)


def post_kernel(x_ref, out_hbm, z_ref, sems):
    sub = lax.broadcasted_iota(jnp.int32, (16, 8, 128), 1)
    sends = []
    for ah in range(8):
        even, odd = x_ref[ah, :, 0], x_ref[ah, :, 1]
        z0 = jnp.where(sub < 4, even, pltpu.roll(odd, 4, 1)).reshape(128, 128)
        z1 = jnp.where(sub < 4, pltpu.roll(even, 4, 1), odd).reshape(128, 128)
        for top, z in enumerate((z0, z1)):
            turned = z.T
            for c in range(2):
                z_ref[c, top, ah] = turned[c * 64 : c * 64 + 64]
        send = pltpu.make_async_copy(z_ref.at[:, :, ah], out_hbm.at[:, :, ah], sems.at[ah])
        send.start()
        sends.append(send)
    for send in sends:
        send.wait()


SMEM = pl.BlockSpec(memory_space=pltpu.SMEM)
VMEM = pl.BlockSpec(memory_space=pltpu.VMEM)
HBM = pl.BlockSpec(memory_space=pltpu.HBM)
PARAMS = pltpu.CompilerParams(vmem_limit_bytes=48 << 20)


def on_device(state_vector, local_gates, local_angles, pair_qubits, pair_angles, group_gates, inner_gate):
    turned = group_gates.transpose(0, 1, 3, 2)
    real, imag = turned[:, 0], turned[:, 1]
    pairs = jnp.concatenate([jnp.concatenate([real, imag], 2), jnp.concatenate([-imag, real], 2)], 1)
    weights = pl.pallas_call(
        prep_kernel,
        out_shape=(
            jax.ShapeDtypeStruct((2, 256, 256), BF16),
            jax.ShapeDtypeStruct((2, 256, 256), BF16),
            jax.ShapeDtypeStruct((128, 256), BF16),
            jax.ShapeDtypeStruct((128, 256), BF16),
            jax.ShapeDtypeStruct((2, 8, 128), F32),
        ),
        in_specs=[SMEM, SMEM, SMEM, VMEM, VMEM],
        out_specs=(VMEM,) * 5,
        compiler_params=PARAMS,
        name="prep",
    )(local_angles, pair_qubits.T, pair_angles, pairs, inner_gate)
    sent = pl.pallas_call(
        pre_kernel,
        out_shape=pltpu.HBM((8, 16, 2, 8, 128), F32),
        in_specs=[HBM, HBM],
        out_specs=HBM,
        scratch_shapes=[
            pltpu.VMEM((2048, 128), F32),
            pltpu.VMEM((2, 2, 32, 32), F32),
            pltpu.VMEM((2048, 128), F32),
            pltpu.VMEM((8, 16, 2, 8, 128), F32),
            pltpu.SemaphoreType.DMA((2,)),
            pltpu.SemaphoreType.DMA((8,)),
        ],
        compiler_params=PARAMS,
        name="pre",
    )(
        pltpu.with_memory_space_constraint(state_vector.reshape(2048, 128), pltpu.HBM),
        pltpu.with_memory_space_constraint(local_gates, pltpu.HBM),
    )
    held = lax.all_to_all(sent.reshape(256, 8, 128), ("grp", "ing"), 0, 0, tiled=True)
    done = pl.pallas_call(
        mid_kernel,
        out_shape=jax.ShapeDtypeStruct((256, 8, 128), F32),
        in_specs=[VMEM] * 6,
        out_specs=VMEM,
        compiler_params=PARAMS,
        name="mid",
    )(held, *weights)
    back = lax.all_to_all(done, ("grp", "ing"), 0, 0, tiled=True)
    out = pl.pallas_call(
        post_kernel,
        out_shape=pltpu.HBM((2, 2, 8, 64, 128), F32),
        in_specs=[VMEM],
        out_specs=HBM,
        scratch_shapes=[pltpu.VMEM((2, 2, 8, 64, 128), F32), pltpu.SemaphoreType.DMA((8,))],
        compiler_params=PARAMS,
        name="post",
    )(back.reshape(8, 16, 2, 8, 128))
    return out.reshape(state_vector.shape)


def solution(mesh):
    return jax.shard_map(
        on_device,
        mesh=mesh,
        in_specs=(P(None, "grp", "ing", None), P(), P(), P(), P(), P(), P()),
        out_specs=P(None, "grp", "ing", None),
        check_vma=False,
    )
```

```python
import jax
import jax.numpy as jnp
from jax import lax
from jax.experimental import pallas as pl
from jax.experimental.pallas import tpu as pltpu
from jax.sharding import PartitionSpec as P

F32 = jnp.float32
BF16 = jnp.bfloat16


def split(value):
    high = value.astype(BF16)
    return high, (value - high.astype(F32)).astype(BF16)


def dot(left, right, dims=((1,), (0,))):
    return lax.dot_general(left, right, (dims, ((), ())), preferred_element_type=F32)


def dot3(left, right, dims=((1,), (0,))):
    (left_high, left_low), (right_high, right_low) = left, right
    return (
        dot(left_high, right_high, dims)
        + dot(left_low, right_high, dims)
        + dot(left_high, right_low, dims)
    )


def prep_kernel(angle_ref, qubit_ref, twist_ref, pair_ref, inner_ref, w_high, w_low, m_high, m_low, turn_ref):
    row = lax.broadcasted_iota(jnp.int32, (256, 8), 0)
    col = lax.broadcasted_iota(jnp.int32, (256, 8), 1)
    r_full = lax.broadcasted_iota(jnp.int32, (256, 256), 0)
    c_full = lax.broadcasted_iota(jnp.int32, (256, 256), 1)
    differ = jnp.bitwise_xor(r_full, c_full)
    for high in range(2):
        halves = []
        for n in range(2):
            level = 2 * high + n
            group = (row >> 7) if n else (row >> 5) & 1
            key = ((row >> 6) & 1) * 4 + group * 2 + ((row >> level) & 1)
            pick = (key == col).astype(F32).astype(BF16)
            others = 255 - (64 + (128 if n else 32) + (1 << level))
            keep = jnp.bitwise_and(differ, others) == 0
            spread = []
            for part in split(pair_ref[level]):
                half = dot(pick, part).astype(BF16)
                spread.append(jnp.where(keep, dot(half, pick, ((1,), (1,))), 0.0).astype(BF16))
            halves.append(spread)
        w_high[high], w_low[high] = split(dot3(*halves))
    row = lax.broadcasted_iota(jnp.int32, (128, 32), 0)
    col = lax.broadcasted_iota(jnp.int32, (128, 32), 1)
    pick = ((row >> 2) == col).astype(F32).astype(BF16)
    keep = jnp.bitwise_and(differ[:128, :128], 3) == 0
    for c in range(2):
        for part, out in zip(split(inner_ref[c]), (m_high, m_low)):
            half = dot(pick, part).astype(BF16)
            out[:, c * 128 : c * 128 + 128] = jnp.where(keep, dot(half, pick, ((1,), (1,))), 0.0).astype(BF16)
    base = (lax.axis_index("grp") & 1) * 64 + lax.axis_index("ing") * 4
    sub = lax.broadcasted_iota(jnp.int32, (8, 128), 0)
    lane = lax.broadcasted_iota(jnp.int32, (8, 128), 1)
    position = ((lane & 7) << 7) + (sub & 3) + base
    phases = jnp.zeros((8, 128), F32)
    for qubit in range(10):
        phases = phases + angle_ref[qubit] * (1 - 2 * ((position >> qubit) & 1)).astype(F32)
    for entry in range(16):
        first_bit = lax.shift_right_logical(position, jnp.full((8, 128), qubit_ref[0, entry], jnp.int32))
        second_bit = lax.shift_right_logical(position, jnp.full((8, 128), qubit_ref[1, entry], jnp.int32))
        odd = jnp.bitwise_and(jnp.bitwise_xor(first_bit, second_bit), 1)
        phases = phases + twist_ref[entry] * (1 - 2 * odd).astype(F32)
    turn_ref[0] = jnp.cos(phases)
    turn_ref[1] = jnp.sin(phases)


def pre_kernel(x_hbm, gate_hbm, out_hbm, x_ref, gate_ref, y_ref, z_ref, in_sems, out_sems):
    fetch_gates = pltpu.make_async_copy(gate_hbm, gate_ref, in_sems.at[0])
    fetch_gates.start()
    fetches = [
        pltpu.make_async_copy(x_hbm.at[pl.ds(1024 * c, 1024)], x_ref.at[pl.ds(1024 * c, 1024)], in_sems.at[1 + c])
        for c in range(2)
    ]
    for fetch in fetches:
        fetch.start()
    fetch_gates.wait()
    real, imag = gate_ref[0, 0], gate_ref[0, 1]
    first = split(jnp.concatenate([jnp.concatenate([real, -imag], 1), jnp.concatenate([imag, real], 1)], 0))
    real, imag = gate_ref[1, 0], gate_ref[1, 1]
    zero = jnp.zeros_like(real)
    rows = [
        [real, zero, -imag, zero],
        [zero, real, zero, -imag],
        [imag, zero, real, zero],
        [zero, imag, zero, real],
    ]
    second = split(jnp.concatenate([jnp.concatenate(r, 1) for r in rows], 0).T)
    first_high, first_low = first
    for c in range(2):
        stacked = jnp.concatenate([m[:, c * 32 : c * 32 + 32] for m in (first_high, first_low, first_high)], 1)
        fetches[c].wait()
        for j in range(4):
            columns = [x_ref[pl.ds(1024 * c + 8 * j + b, 32, stride=32), :] for b in range(8)]
            high, rest = split(jnp.concatenate(columns, 1))
            result = dot(stacked, jnp.concatenate([high, high, rest], 0))
            for b in range(8):
                at = (8 * j + b) * 64
                value = result[:, b * 128 : b * 128 + 128]
                y_ref[at : at + 64] = value if c == 0 else y_ref[at : at + 64] + value
    sub = lax.broadcasted_iota(jnp.int32, (16, 8, 128), 1)
    sends = []
    for ah in range(8):
        halves = []
        for top in range(2):
            a = (top * 8 + ah) * 2
            x = jnp.concatenate([y_ref[pl.ds(c * 32 + a + q, 32, stride=64), :] for c in range(2) for q in range(2)], 0)
            halves.append(dot3(split(x.T), second).reshape(16, 8, 128))
        z0, z1 = halves
        z_ref[ah, :, 0] = jnp.where(sub < 4, z0, pltpu.roll(z1, 4, 1))
        z_ref[ah, :, 1] = jnp.where(sub < 4, pltpu.roll(z0, 4, 1), z1)
        sends.append(pltpu.make_async_copy(z_ref.at[ah], out_hbm.at[ah], out_sems.at[ah]))
        sends[-1].start()
    for send in sends:
        send.wait()


def mid_kernel(x_ref, w_high, w_low, m_high, m_low, turn_ref, out_ref):
    inner = (m_high[...], m_low[...])
    lane = lax.broadcasted_iota(jnp.int32, (128, 128), 1)
    cosine, sine = turn_ref[0], turn_ref[1]
    sign = jnp.where(lane[:8] < 64, -1.0, 1.0)
    cosine_i, sine_i = cosine * sign, sine * sign
    parts = []
    for start in range(0, 16, 2):
        columns = []
        for g in range(start, start + 2):
            x = x_ref[g * 16 : g * 16 + 16]
            swapped = pltpu.roll(x.reshape(128, 128), 64, 1).reshape(16, 8, 128)
            third = cosine * x + sine_i * swapped
            third_i = cosine_i * swapped - sine * x
            columns.append(jnp.concatenate([third.reshape(128, 128), third_i.reshape(128, 128)], 0))
        u = dot3(inner, split(jnp.concatenate(columns, 1)))
        parts += [u[:, :128], u[:, 128:]]
    low = (lane & 32) == 0

    def trade(first, second):
        return (
            jnp.where(low, first, pltpu.roll(second, 32, 1)),
            jnp.where(low, pltpu.roll(first, 96, 1), second),
        )

    def join(pairs, level):
        for start in range(0, 8, 2):
            some = pairs[start : start + 2]
            left = jnp.concatenate([jnp.concatenate([parts[g], parts[h]], 1) for g, h in some], 0)
            y = dot3(split(left), (w_high[level], w_low[level]))
            for n, (g, h) in enumerate(some):
                rows = y[n * 128 : n * 128 + 128]
                parts[g], parts[h] = rows[:, :128], rows[:, 128:]

    for g in range(0, 16, 2):
        parts[g], parts[g + 1] = trade(parts[g], parts[g + 1])
    join([(g, g + 2) for g in (0, 1, 4, 5, 8, 9, 12, 13)], 0)
    for g in (0, 1, 2, 3, 8, 9, 10, 11):
        parts[g], parts[g + 4] = trade(parts[g], parts[g + 4])
    join([(g, g + 8) for g in range(8)], 1)
    for g in range(0, 16, 2):
        parts[g], parts[g + 1] = trade(parts[g], parts[g + 1])
    for slot in range(16):
        g = (slot & 8) | (slot & 2) | ((slot & 1) << 2) | ((slot >> 2) & 1)
        out_ref[g * 16 : g * 16 + 16] = parts[slot].reshape(16, 8, 128)


def post_kernel(x_ref, out_hbm, z_ref, sems):
    sub = lax.broadcasted_iota(jnp.int32, (16, 8, 128), 1)
    sends = []
    for ah in range(8):
        even, odd = x_ref[ah, :, 0], x_ref[ah, :, 1]
        z0 = jnp.where(sub < 4, even, pltpu.roll(odd, 4, 1)).reshape(128, 128)
        z1 = jnp.where(sub < 4, pltpu.roll(even, 4, 1), odd).reshape(128, 128)
        for top, z in enumerate((z0, z1)):
            turned = z.T
            for c in range(2):
                z_ref[c, top, ah] = turned[c * 64 : c * 64 + 64]
        send = pltpu.make_async_copy(z_ref.at[:, :, ah], out_hbm.at[:, :, ah], sems.at[ah])
        send.start()
        sends.append(send)
    for send in sends:
        send.wait()


SMEM = pl.BlockSpec(memory_space=pltpu.SMEM)
VMEM = pl.BlockSpec(memory_space=pltpu.VMEM)
HBM = pl.BlockSpec(memory_space=pltpu.HBM)
PARAMS = pltpu.CompilerParams(vmem_limit_bytes=48 << 20)


def on_device(state_vector, local_gates, local_angles, pair_qubits, pair_angles, group_gates, inner_gate):
    turned = group_gates.transpose(0, 1, 3, 2)
    real, imag = turned[:, 0], turned[:, 1]
    pairs = jnp.concatenate([jnp.concatenate([real, imag], 2), jnp.concatenate([-imag, real], 2)], 1)
    weights = pl.pallas_call(
        prep_kernel,
        out_shape=(
            jax.ShapeDtypeStruct((2, 256, 256), BF16),
            jax.ShapeDtypeStruct((2, 256, 256), BF16),
            jax.ShapeDtypeStruct((128, 256), BF16),
            jax.ShapeDtypeStruct((128, 256), BF16),
            jax.ShapeDtypeStruct((2, 8, 128), F32),
        ),
        in_specs=[SMEM, SMEM, SMEM, VMEM, VMEM],
        out_specs=(VMEM,) * 5,
        compiler_params=PARAMS,
        name="prep",
    )(local_angles, pair_qubits.T, pair_angles, pairs, inner_gate)
    sent = pl.pallas_call(
        pre_kernel,
        out_shape=pltpu.HBM((8, 16, 2, 8, 128), F32),
        in_specs=[HBM, HBM],
        out_specs=HBM,
        scratch_shapes=[
            pltpu.VMEM((2048, 128), F32),
            pltpu.VMEM((2, 2, 32, 32), F32),
            pltpu.VMEM((2048, 128), F32),
            pltpu.VMEM((8, 16, 2, 8, 128), F32),
            pltpu.SemaphoreType.DMA((3,)),
            pltpu.SemaphoreType.DMA((8,)),
        ],
        compiler_params=PARAMS,
        name="pre",
    )(
        pltpu.with_memory_space_constraint(state_vector.reshape(2048, 128), pltpu.HBM),
        pltpu.with_memory_space_constraint(local_gates, pltpu.HBM),
    )
    held = lax.all_to_all(sent.reshape(256, 8, 128), ("grp", "ing"), 0, 0, tiled=True)
    done = pl.pallas_call(
        mid_kernel,
        out_shape=jax.ShapeDtypeStruct((256, 8, 128), F32),
        in_specs=[VMEM] * 6,
        out_specs=VMEM,
        compiler_params=PARAMS,
        name="mid",
    )(held, *weights)
    back = lax.all_to_all(done, ("grp", "ing"), 0, 0, tiled=True)
    out = pl.pallas_call(
        post_kernel,
        out_shape=pltpu.HBM((2, 2, 8, 64, 128), F32),
        in_specs=[VMEM],
        out_specs=HBM,
        scratch_shapes=[pltpu.VMEM((2, 2, 8, 64, 128), F32), pltpu.SemaphoreType.DMA((8,))],
        compiler_params=PARAMS,
        name="post",
    )(back.reshape(8, 16, 2, 8, 128))
    return out.reshape(state_vector.shape)


def solution(mesh):
    return jax.shard_map(
        on_device,
        mesh=mesh,
        in_specs=(P(None, "grp", "ing", None), P(), P(), P(), P(), P(), P()),
        out_specs=P(None, "grp", "ing", None),
        check_vma=False,
    )
```

```python
import jax
import jax.numpy as jnp
from jax import lax
from jax.experimental import pallas as pl
from jax.experimental.pallas import tpu as pltpu
from jax.sharding import PartitionSpec as P

F32 = jnp.float32
BF16 = jnp.bfloat16


def split(value):
    high = value.astype(BF16)
    return high, (value - high.astype(F32)).astype(BF16)


def dot(left, right, dims=((1,), (0,))):
    return lax.dot_general(left, right, (dims, ((), ())), preferred_element_type=F32)


def dot3(left, right, dims=((1,), (0,))):
    (left_high, left_low), (right_high, right_low) = left, right
    return (
        dot(left_high, right_high, dims)
        + dot(left_low, right_high, dims)
        + dot(left_high, right_low, dims)
    )


def prep_kernel(angle_ref, qubit_ref, twist_ref, pair_ref, inner_ref, w_high, w_low, m_high, m_low, turn_ref):
    row = lax.broadcasted_iota(jnp.int32, (256, 8), 0)
    col = lax.broadcasted_iota(jnp.int32, (256, 8), 1)
    r_full = lax.broadcasted_iota(jnp.int32, (256, 256), 0)
    c_full = lax.broadcasted_iota(jnp.int32, (256, 256), 1)
    differ = jnp.bitwise_xor(r_full, c_full)
    for high in range(2):
        halves = []
        for n in range(2):
            level = 2 * high + n
            group = (row >> 7) if n else (row >> 5) & 1
            key = ((row >> 6) & 1) * 4 + group * 2 + ((row >> level) & 1)
            pick = (key == col).astype(F32).astype(BF16)
            others = 255 - (64 + (128 if n else 32) + (1 << level))
            keep = jnp.bitwise_and(differ, others) == 0
            spread = []
            for part in split(pair_ref[level]):
                half = dot(pick, part).astype(BF16)
                spread.append(jnp.where(keep, dot(half, pick, ((1,), (1,))), 0.0).astype(BF16))
            halves.append(spread)
        w_high[high], w_low[high] = split(dot3(*halves))
    row = lax.broadcasted_iota(jnp.int32, (128, 32), 0)
    col = lax.broadcasted_iota(jnp.int32, (128, 32), 1)
    pick = ((row >> 2) == col).astype(F32).astype(BF16)
    keep = jnp.bitwise_and(differ[:128, :128], 3) == 0
    for c in range(2):
        for part, out in zip(split(inner_ref[c]), (m_high, m_low)):
            half = dot(pick, part).astype(BF16)
            out[:, c * 128 : c * 128 + 128] = jnp.where(keep, dot(half, pick, ((1,), (1,))), 0.0).astype(BF16)
    base = (lax.axis_index("grp") & 1) * 64 + lax.axis_index("ing") * 4
    sub = lax.broadcasted_iota(jnp.int32, (8, 128), 0)
    lane = lax.broadcasted_iota(jnp.int32, (8, 128), 1)
    position = ((lane & 7) << 7) + (sub & 3) + base
    phases = jnp.zeros((8, 128), F32)
    for qubit in range(10):
        phases = phases + angle_ref[qubit] * (1 - 2 * ((position >> qubit) & 1)).astype(F32)
    for entry in range(16):
        first_bit = lax.shift_right_logical(position, jnp.full((8, 128), qubit_ref[0, entry], jnp.int32))
        second_bit = lax.shift_right_logical(position, jnp.full((8, 128), qubit_ref[1, entry], jnp.int32))
        odd = jnp.bitwise_and(jnp.bitwise_xor(first_bit, second_bit), 1)
        phases = phases + twist_ref[entry] * (1 - 2 * odd).astype(F32)
    turn_ref[0] = jnp.cos(phases)
    turn_ref[1] = jnp.sin(phases)


def pre_kernel(x_hbm, gate_hbm, out_hbm, x_ref, gate_ref, y_ref, z_ref, in_sems, out_sems):
    fetch_gates = pltpu.make_async_copy(gate_hbm, gate_ref, in_sems.at[0])
    fetch_gates.start()
    fetches = [
        pltpu.make_async_copy(x_hbm.at[pl.ds(1024 * c, 1024)], x_ref.at[pl.ds(1024 * c, 1024)], in_sems.at[1 + c])
        for c in range(2)
    ]
    for fetch in fetches:
        fetch.start()
    fetch_gates.wait()
    real, imag = gate_ref[0, 0], gate_ref[0, 1]
    first = split(jnp.concatenate([jnp.concatenate([real, -imag], 1), jnp.concatenate([imag, real], 1)], 0))
    real, imag = gate_ref[1, 0], gate_ref[1, 1]
    zero = jnp.zeros_like(real)
    rows = [
        [real, zero, -imag, zero],
        [zero, real, zero, -imag],
        [imag, zero, real, zero],
        [zero, imag, zero, real],
    ]
    second = split(jnp.concatenate([jnp.concatenate(r, 1) for r in rows], 0).T)
    first_high, first_low = first
    for c in range(2):
        stacked = jnp.concatenate([m[:, c * 32 : c * 32 + 32] for m in (first_high, first_low, first_high)], 1)
        fetches[c].wait()
        for j in range(4):
            columns = [x_ref[pl.ds(1024 * c + 8 * j + b, 32, stride=32), :] for b in range(8)]
            high, rest = split(jnp.concatenate(columns, 1))
            result = dot(stacked, jnp.concatenate([high, high, rest], 0))
            for b in range(8):
                at = (8 * j + b) * 64
                value = result[:, b * 128 : b * 128 + 128]
                y_ref[at : at + 64] = value if c == 0 else y_ref[at : at + 64] + value
    sub = lax.broadcasted_iota(jnp.int32, (16, 8, 128), 1)
    sends = []
    for ah in range(8):
        halves = []
        for top in range(2):
            a = (top * 8 + ah) * 2
            x = jnp.concatenate([y_ref[pl.ds(c * 32 + a + q, 32, stride=64), :] for c in range(2) for q in range(2)], 0)
            halves.append(dot3(split(x.T), second).reshape(16, 8, 128))
        z0, z1 = halves
        z_ref[ah, :, 0] = jnp.where(sub < 4, z0, pltpu.roll(z1, 4, 1))
        z_ref[ah, :, 1] = jnp.where(sub < 4, pltpu.roll(z0, 4, 1), z1)
        sends.append(pltpu.make_async_copy(z_ref.at[ah], out_hbm.at[ah], out_sems.at[ah]))
        sends[-1].start()
    for send in sends:
        send.wait()


def mid_kernel(x_ref, w_high, w_low, m_high, m_low, turn_ref, out_ref):
    inner = (m_high[...], m_low[...])
    lane = lax.broadcasted_iota(jnp.int32, (128, 128), 1)
    cosine, sine = turn_ref[0], turn_ref[1]
    sign = jnp.where(lane[:8] < 64, -1.0, 1.0)
    cosine_i, sine_i = cosine * sign, sine * sign
    parts = []
    for start in range(0, 16, 2):
        columns = []
        for g in range(start, start + 2):
            x = x_ref[g * 16 : g * 16 + 16]
            swapped = pltpu.roll(x.reshape(128, 128), 64, 1).reshape(16, 8, 128)
            third = cosine * x + sine_i * swapped
            third_i = cosine_i * swapped - sine * x
            columns.append(jnp.concatenate([third.reshape(128, 128), third_i.reshape(128, 128)], 0))
        u = dot3(inner, split(jnp.concatenate(columns, 1)))
        parts += [u[:, :128], u[:, 128:]]
    low = (lane & 32) == 0

    def trade(first, second):
        return (
            jnp.where(low, first, pltpu.roll(second, 32, 1)),
            jnp.where(low, pltpu.roll(first, 96, 1), second),
        )

    def join(pairs, level):
        for start in range(0, 8, 2):
            some = pairs[start : start + 2]
            left = jnp.concatenate([jnp.concatenate([parts[g], parts[h]], 1) for g, h in some], 0)
            y = dot3(split(left), (w_high[level], w_low[level]))
            for n, (g, h) in enumerate(some):
                rows = y[n * 128 : n * 128 + 128]
                parts[g], parts[h] = rows[:, :128], rows[:, 128:]

    for g in range(0, 16, 2):
        parts[g], parts[g + 1] = trade(parts[g], parts[g + 1])
    join([(g, g + 2) for g in (0, 1, 4, 5, 8, 9, 12, 13)], 0)
    for g in (0, 1, 2, 3, 8, 9, 10, 11):
        parts[g], parts[g + 4] = trade(parts[g], parts[g + 4])
    join([(g, g + 8) for g in range(8)], 1)
    for g in range(0, 16, 2):
        parts[g], parts[g + 1] = trade(parts[g], parts[g + 1])
    for slot in range(16):
        g = (slot & 8) | (slot & 2) | ((slot & 1) << 2) | ((slot >> 2) & 1)
        out_ref[g * 16 : g * 16 + 16] = parts[slot].reshape(16, 8, 128)


def post_kernel(x_ref, out_hbm, z_ref, sems):
    sub = lax.broadcasted_iota(jnp.int32, (16, 8, 128), 1)
    sends = []
    for ah in range(8):
        even, odd = x_ref[ah, :, 0], x_ref[ah, :, 1]
        z0 = jnp.where(sub < 4, even, pltpu.roll(odd, 4, 1)).reshape(128, 128)
        z1 = jnp.where(sub < 4, pltpu.roll(even, 4, 1), odd).reshape(128, 128)
        for top, z in enumerate((z0, z1)):
            turned = z.T
            for c in range(2):
                z_ref[c, top, ah] = turned[c * 64 : c * 64 + 64]
            send = pltpu.make_async_copy(z_ref.at[:, top, ah], out_hbm.at[:, top, ah], sems.at[2 * ah + top])
            send.start()
            sends.append(send)
    for send in sends:
        send.wait()


SMEM = pl.BlockSpec(memory_space=pltpu.SMEM)
VMEM = pl.BlockSpec(memory_space=pltpu.VMEM)
HBM = pl.BlockSpec(memory_space=pltpu.HBM)
PARAMS = pltpu.CompilerParams(vmem_limit_bytes=48 << 20)


def on_device(state_vector, local_gates, local_angles, pair_qubits, pair_angles, group_gates, inner_gate):
    turned = group_gates.transpose(0, 1, 3, 2)
    real, imag = turned[:, 0], turned[:, 1]
    pairs = jnp.concatenate([jnp.concatenate([real, imag], 2), jnp.concatenate([-imag, real], 2)], 1)
    weights = pl.pallas_call(
        prep_kernel,
        out_shape=(
            jax.ShapeDtypeStruct((2, 256, 256), BF16),
            jax.ShapeDtypeStruct((2, 256, 256), BF16),
            jax.ShapeDtypeStruct((128, 256), BF16),
            jax.ShapeDtypeStruct((128, 256), BF16),
            jax.ShapeDtypeStruct((2, 8, 128), F32),
        ),
        in_specs=[SMEM, SMEM, SMEM, VMEM, VMEM],
        out_specs=(VMEM,) * 5,
        compiler_params=PARAMS,
        name="prep",
    )(local_angles, pair_qubits.T, pair_angles, pairs, inner_gate)
    sent = pl.pallas_call(
        pre_kernel,
        out_shape=pltpu.HBM((8, 16, 2, 8, 128), F32),
        in_specs=[HBM, HBM],
        out_specs=HBM,
        scratch_shapes=[
            pltpu.VMEM((2048, 128), F32),
            pltpu.VMEM((2, 2, 32, 32), F32),
            pltpu.VMEM((2048, 128), F32),
            pltpu.VMEM((8, 16, 2, 8, 128), F32),
            pltpu.SemaphoreType.DMA((3,)),
            pltpu.SemaphoreType.DMA((8,)),
        ],
        compiler_params=PARAMS,
        name="pre",
    )(
        pltpu.with_memory_space_constraint(state_vector.reshape(2048, 128), pltpu.HBM),
        pltpu.with_memory_space_constraint(local_gates, pltpu.HBM),
    )
    held = lax.all_to_all(sent.reshape(256, 8, 128), ("grp", "ing"), 0, 0, tiled=True)
    done = pl.pallas_call(
        mid_kernel,
        out_shape=jax.ShapeDtypeStruct((256, 8, 128), F32),
        in_specs=[VMEM] * 6,
        out_specs=VMEM,
        compiler_params=PARAMS,
        name="mid",
    )(held, *weights)
    back = lax.all_to_all(done, ("grp", "ing"), 0, 0, tiled=True)
    out = pl.pallas_call(
        post_kernel,
        out_shape=pltpu.HBM((2, 2, 8, 64, 128), F32),
        in_specs=[VMEM],
        out_specs=HBM,
        scratch_shapes=[pltpu.VMEM((2, 2, 8, 64, 128), F32), pltpu.SemaphoreType.DMA((16,))],
        compiler_params=PARAMS,
        name="post",
    )(back.reshape(8, 16, 2, 8, 128))
    return out.reshape(state_vector.shape)


def solution(mesh):
    return jax.shard_map(
        on_device,
        mesh=mesh,
        in_specs=(P(None, "grp", "ing", None), P(), P(), P(), P(), P(), P()),
        out_specs=P(None, "grp", "ing", None),
        check_vma=False,
    )
```

```python
import jax
import jax.numpy as jnp
from jax import lax
from jax.experimental import pallas as pl
from jax.experimental.pallas import tpu as pltpu
from jax.sharding import PartitionSpec as P

F32 = jnp.float32
BF16 = jnp.bfloat16


def split(value):
    high = value.astype(BF16)
    return high, (value - high.astype(F32)).astype(BF16)


def dot(left, right, dims=((1,), (0,))):
    return lax.dot_general(left, right, (dims, ((), ())), preferred_element_type=F32)


def dot3(left, right, dims=((1,), (0,))):
    (left_high, left_low), (right_high, right_low) = left, right
    return (
        dot(left_high, right_high, dims)
        + dot(left_low, right_high, dims)
        + dot(left_high, right_low, dims)
    )


def prep_kernel(angle_ref, qubit_ref, twist_ref, pair_ref, inner_ref, w_high, w_low, m_high, m_low, turn_ref):
    row = lax.broadcasted_iota(jnp.int32, (256, 8), 0)
    col = lax.broadcasted_iota(jnp.int32, (256, 8), 1)
    r_full = lax.broadcasted_iota(jnp.int32, (256, 256), 0)
    c_full = lax.broadcasted_iota(jnp.int32, (256, 256), 1)
    differ = jnp.bitwise_xor(r_full, c_full)
    for high in range(2):
        halves = []
        for n in range(2):
            level = 2 * high + n
            group = (row >> 7) if n else (row >> 5) & 1
            key = ((row >> 6) & 1) * 4 + group * 2 + ((row >> level) & 1)
            pick = (key == col).astype(F32).astype(BF16)
            others = 255 - (64 + (128 if n else 32) + (1 << level))
            keep = jnp.bitwise_and(differ, others) == 0
            spread = []
            for part in split(pair_ref[level]):
                half = dot(pick, part).astype(BF16)
                spread.append(jnp.where(keep, dot(half, pick, ((1,), (1,))), 0.0).astype(BF16))
            halves.append(spread)
        w_high[high], w_low[high] = split(dot3(*halves))
    row = lax.broadcasted_iota(jnp.int32, (128, 32), 0)
    col = lax.broadcasted_iota(jnp.int32, (128, 32), 1)
    pick = ((row >> 2) == col).astype(F32).astype(BF16)
    keep = jnp.bitwise_and(differ[:128, :128], 3) == 0
    for c in range(2):
        for part, out in zip(split(inner_ref[c]), (m_high, m_low)):
            half = dot(pick, part).astype(BF16)
            out[:, c * 128 : c * 128 + 128] = jnp.where(keep, dot(half, pick, ((1,), (1,))), 0.0).astype(BF16)
    base = (lax.axis_index("grp") & 1) * 64 + lax.axis_index("ing") * 4
    sub = lax.broadcasted_iota(jnp.int32, (8, 128), 0)
    lane = lax.broadcasted_iota(jnp.int32, (8, 128), 1)
    position = ((lane & 7) << 7) + (sub & 3) + base
    phases = jnp.zeros((8, 128), F32)
    for qubit in range(10):
        phases = phases + angle_ref[qubit] * (1 - 2 * ((position >> qubit) & 1)).astype(F32)
    for entry in range(16):
        first_bit = lax.shift_right_logical(position, jnp.full((8, 128), qubit_ref[0, entry], jnp.int32))
        second_bit = lax.shift_right_logical(position, jnp.full((8, 128), qubit_ref[1, entry], jnp.int32))
        odd = jnp.bitwise_and(jnp.bitwise_xor(first_bit, second_bit), 1)
        phases = phases + twist_ref[entry] * (1 - 2 * odd).astype(F32)
    turn_ref[0] = jnp.cos(phases)
    turn_ref[1] = jnp.sin(phases)


def pre_kernel(x_hbm, gate_hbm, out_hbm, x_ref, gate_ref, y_ref, z_ref, in_sems, out_sems):
    fetch_gates = pltpu.make_async_copy(gate_hbm, gate_ref, in_sems.at[0])
    fetch_gates.start()
    fetches = [
        pltpu.make_async_copy(x_hbm.at[pl.ds(1024 * c, 1024)], x_ref.at[pl.ds(1024 * c, 1024)], in_sems.at[1 + c])
        for c in range(2)
    ]
    for fetch in fetches:
        fetch.start()
    fetch_gates.wait()
    real, imag = gate_ref[0, 0], gate_ref[0, 1]
    first = split(jnp.concatenate([jnp.concatenate([real, -imag], 1), jnp.concatenate([imag, real], 1)], 0))
    first_high, first_low = first
    for c in range(2):
        if c == 1:
            real, imag = gate_ref[1, 0], gate_ref[1, 1]
            zero = jnp.zeros_like(real)
            rows = [
                [real, zero, -imag, zero],
                [zero, real, zero, -imag],
                [imag, zero, real, zero],
                [zero, imag, zero, real],
            ]
            second = split(jnp.concatenate([jnp.concatenate(r, 1) for r in rows], 0).T)
        stacked = jnp.concatenate([m[:, c * 32 : c * 32 + 32] for m in (first_high, first_low, first_high)], 1)
        fetches[c].wait()
        for j in range(4):
            columns = [x_ref[pl.ds(1024 * c + 8 * j + b, 32, stride=32), :] for b in range(8)]
            high, rest = split(jnp.concatenate(columns, 1))
            result = dot(stacked, jnp.concatenate([high, high, rest], 0))
            for b in range(8):
                at = (8 * j + b) * 64
                value = result[:, b * 128 : b * 128 + 128]
                y_ref[at : at + 64] = value if c == 0 else y_ref[at : at + 64] + value
    sub = lax.broadcasted_iota(jnp.int32, (16, 8, 128), 1)
    sends = []
    for ah in range(8):
        halves = []
        for top in range(2):
            a = (top * 8 + ah) * 2
            x = jnp.concatenate([y_ref[pl.ds(c * 32 + a + q, 32, stride=64), :] for c in range(2) for q in range(2)], 0)
            halves.append(dot3(split(x.T), second).reshape(16, 8, 128))
        z0, z1 = halves
        z_ref[ah, :, 0] = jnp.where(sub < 4, z0, pltpu.roll(z1, 4, 1))
        z_ref[ah, :, 1] = jnp.where(sub < 4, pltpu.roll(z0, 4, 1), z1)
        sends.append(pltpu.make_async_copy(z_ref.at[ah], out_hbm.at[ah], out_sems.at[ah]))
        sends[-1].start()
    for send in sends:
        send.wait()


def mid_kernel(x_ref, w_high, w_low, m_high, m_low, turn_ref, out_ref):
    inner = (m_high[...], m_low[...])
    lane = lax.broadcasted_iota(jnp.int32, (128, 128), 1)
    cosine, sine = turn_ref[0], turn_ref[1]
    sign = jnp.where(lane[:8] < 64, -1.0, 1.0)
    cosine_i, sine_i = cosine * sign, sine * sign
    parts = []
    for start in range(0, 16, 2):
        columns = []
        for g in range(start, start + 2):
            x = x_ref[g * 16 : g * 16 + 16]
            swapped = pltpu.roll(x.reshape(128, 128), 64, 1).reshape(16, 8, 128)
            third = cosine * x + sine_i * swapped
            third_i = cosine_i * swapped - sine * x
            columns.append(jnp.concatenate([third.reshape(128, 128), third_i.reshape(128, 128)], 0))
        u = dot3(inner, split(jnp.concatenate(columns, 1)))
        parts += [u[:, :128], u[:, 128:]]
    low = (lane & 32) == 0

    def trade(first, second):
        return (
            jnp.where(low, first, pltpu.roll(second, 32, 1)),
            jnp.where(low, pltpu.roll(first, 96, 1), second),
        )

    def join(pairs, level):
        for start in range(0, 8, 2):
            some = pairs[start : start + 2]
            left = jnp.concatenate([jnp.concatenate([parts[g], parts[h]], 1) for g, h in some], 0)
            y = dot3(split(left), (w_high[level], w_low[level]))
            for n, (g, h) in enumerate(some):
                rows = y[n * 128 : n * 128 + 128]
                parts[g], parts[h] = rows[:, :128], rows[:, 128:]

    for g in range(0, 16, 2):
        parts[g], parts[g + 1] = trade(parts[g], parts[g + 1])
    join([(g, g + 2) for g in (0, 1, 4, 5, 8, 9, 12, 13)], 0)
    for g in (0, 1, 2, 3, 8, 9, 10, 11):
        parts[g], parts[g + 4] = trade(parts[g], parts[g + 4])
    join([(g, g + 8) for g in range(8)], 1)
    for g in range(0, 16, 2):
        parts[g], parts[g + 1] = trade(parts[g], parts[g + 1])
    for slot in range(16):
        g = (slot & 8) | (slot & 2) | ((slot & 1) << 2) | ((slot >> 2) & 1)
        out_ref[g * 16 : g * 16 + 16] = parts[slot].reshape(16, 8, 128)


def post_kernel(x_ref, out_hbm, z_ref, sems):
    sub = lax.broadcasted_iota(jnp.int32, (16, 8, 128), 1)
    sends = []
    for ah in range(8):
        even, odd = x_ref[ah, :, 0], x_ref[ah, :, 1]
        z0 = jnp.where(sub < 4, even, pltpu.roll(odd, 4, 1)).reshape(128, 128)
        z1 = jnp.where(sub < 4, pltpu.roll(even, 4, 1), odd).reshape(128, 128)
        for top, z in enumerate((z0, z1)):
            turned = z.T
            for c in range(2):
                z_ref[c, top, ah] = turned[c * 64 : c * 64 + 64]
            send = pltpu.make_async_copy(z_ref.at[:, top, ah], out_hbm.at[:, top, ah], sems.at[2 * ah + top])
            send.start()
            sends.append(send)
    for send in sends:
        send.wait()


SMEM = pl.BlockSpec(memory_space=pltpu.SMEM)
VMEM = pl.BlockSpec(memory_space=pltpu.VMEM)
HBM = pl.BlockSpec(memory_space=pltpu.HBM)
PARAMS = pltpu.CompilerParams(vmem_limit_bytes=48 << 20)


def on_device(state_vector, local_gates, local_angles, pair_qubits, pair_angles, group_gates, inner_gate):
    turned = group_gates.transpose(0, 1, 3, 2)
    real, imag = turned[:, 0], turned[:, 1]
    pairs = jnp.concatenate([jnp.concatenate([real, imag], 2), jnp.concatenate([-imag, real], 2)], 1)
    weights = pl.pallas_call(
        prep_kernel,
        out_shape=(
            jax.ShapeDtypeStruct((2, 256, 256), BF16),
            jax.ShapeDtypeStruct((2, 256, 256), BF16),
            jax.ShapeDtypeStruct((128, 256), BF16),
            jax.ShapeDtypeStruct((128, 256), BF16),
            jax.ShapeDtypeStruct((2, 8, 128), F32),
        ),
        in_specs=[SMEM, SMEM, SMEM, VMEM, VMEM],
        out_specs=(VMEM,) * 5,
        compiler_params=PARAMS,
        name="prep",
    )(local_angles, pair_qubits.T, pair_angles, pairs, inner_gate)
    sent = pl.pallas_call(
        pre_kernel,
        out_shape=pltpu.HBM((8, 16, 2, 8, 128), F32),
        in_specs=[HBM, HBM],
        out_specs=HBM,
        scratch_shapes=[
            pltpu.VMEM((2048, 128), F32),
            pltpu.VMEM((2, 2, 32, 32), F32),
            pltpu.VMEM((2048, 128), F32),
            pltpu.VMEM((8, 16, 2, 8, 128), F32),
            pltpu.SemaphoreType.DMA((3,)),
            pltpu.SemaphoreType.DMA((8,)),
        ],
        compiler_params=PARAMS,
        name="pre",
    )(
        pltpu.with_memory_space_constraint(state_vector.reshape(2048, 128), pltpu.HBM),
        pltpu.with_memory_space_constraint(local_gates, pltpu.HBM),
    )
    held = lax.all_to_all(sent.reshape(256, 8, 128), ("grp", "ing"), 0, 0, tiled=True)
    done = pl.pallas_call(
        mid_kernel,
        out_shape=jax.ShapeDtypeStruct((256, 8, 128), F32),
        in_specs=[VMEM] * 6,
        out_specs=VMEM,
        compiler_params=PARAMS,
        name="mid",
    )(held, *weights)
    back = lax.all_to_all(done, ("grp", "ing"), 0, 0, tiled=True)
    out = pl.pallas_call(
        post_kernel,
        out_shape=pltpu.HBM((2, 2, 8, 64, 128), F32),
        in_specs=[VMEM],
        out_specs=HBM,
        scratch_shapes=[pltpu.VMEM((2, 2, 8, 64, 128), F32), pltpu.SemaphoreType.DMA((16,))],
        compiler_params=PARAMS,
        name="post",
    )(back.reshape(8, 16, 2, 8, 128))
    return out.reshape(state_vector.shape)


def solution(mesh):
    return jax.shard_map(
        on_device,
        mesh=mesh,
        in_specs=(P(None, "grp", "ing", None), P(), P(), P(), P(), P(), P()),
        out_specs=P(None, "grp", "ing", None),
        check_vma=False,
    )
```
